32 devices in a mesh: gx: 4 (over z), gy: 4 (over x, core), gz: 2 (over y).
Axes of the slice: x: 2, y: 2, z: 4, core: 2. Of those that a mesh axis runs over, the one named last changes fastest.
Arguments:
- hidden: bfloat16 [12288, 4608], P(('gx', 'gy', 'gz')), may hold values from -6 to 6
- out_grad: bfloat16 [12288, 1152], P(('gx', 'gy', 'gz')), may hold values from -6 to 6
- down_weight: bfloat16 [4608, 1152], replicated, may hold values from -0.1875 to 0.1875
Outputs:
- weight_grad: float32 [4608, 1152], P(('gx', 'gy', 'gz'))
- hidden_grad: bfloat16 [12288, 4608], P(('gx', 'gy', 'gz'))
The draws below stay inside these ranges and needn't reach their ends.
All inputs are finite; a program needn't handle non-finite values.
Results may differ from the reference program's by a relative error of at most 0.001.
Values may be sent and summed in bfloat16 or wider, within the bound.
A program may use at most 128 MiB of HBM per device.

```python
import jax
import jax.numpy as jnp
from jax import lax

FFW = 4608
DW = 1152
TOKENS = 12288


def strengthened(array, rng, source, target, shards_of, factor):
    owner, partner = [(jnp.arange(array.shape[dim]) // (array.shape[dim] // shards_of)).reshape([-1 if axis == dim else 1 for axis in range(array.ndim)]) for dim in (source, target)]
    chosen = jax.random.permutation(rng, shards_of)[partner]
    strong = (owner == chosen) | (owner == (partner + shards_of // 2) % shards_of)
    return jnp.where(strong, factor * array, array)


def block_scale(rng, dims, split, least, largest):
    level = 1.0
    for axis_at, shards_of in split:
        draws = jax.random.uniform(jax.random.fold_in(jax.random.fold_in(rng, 6), axis_at), (shards_of,), jnp.float32, least / len(split), largest / len(split))
        level = level * jnp.repeat(jnp.exp(draws), dims[axis_at] // shards_of).reshape((-1,) + (1,) * (len(dims) - 1 - axis_at))
    return level


def centred(own_key, dims, width, most, cuts=(), kind=jnp.bfloat16):
    drawn = jax.random.normal(own_key, dims, jnp.float32) * width
    if len(cuts) > 0:
        drawn = block_scale(own_key, dims, cuts, -0.22, 0.18) * drawn
    return jnp.clip(drawn, min=-most, max=most).astype(kind)


def heavy_noise(rng, shape, deviation, reach, cuts, heavy, kind=jnp.bfloat16):
    values = deviation * jax.random.normal(rng, shape, jnp.float32)
    if cuts:
        values = values * block_scale(rng, shape, cuts, -0.22, 0.18)
    return jnp.clip(strengthened(values, jax.random.fold_in(rng, 3), *heavy), -reach, reach).astype(kind)


def setup_inputs(seed: int = 0) -> dict:
    splits = jax.random.split(jax.random.key(seed), 4)
    hidden = heavy_noise(splits[0], (TOKENS, FFW), 1.0, 6.0, ((0, 32),), (0, 1, 32, 2.75))
    out_grad = centred(splits[1], (TOKENS, DW), 1.0, 6.0, ((0, 32),))
    down_weight = centred(splits[2], (FFW, DW), DW ** -0.5, 0.1875)
    return {"hidden": hidden, "out_grad": out_grad, "down_weight": down_weight}


def reference(hidden, out_grad, down_weight):
    summed = lax.dot_general(hidden, out_grad, (((0,), (0,)), ((), ())), preferred_element_type=jnp.float32)
    weight_grad = summed / jnp.sqrt(jnp.float32(TOKENS))
    hidden_grad = lax.dot_general(out_grad, down_weight, (((1,), (1,)), ((), ())), preferred_element_type=jnp.float32)
    return (weight_grad, hidden_grad.astype(jnp.bfloat16))
```

```python
import functools

import jax
import jax.numpy as jnp
from jax import lax
from jax.experimental import pallas as pl
from jax.experimental.pallas import tpu as pltpu
from jax.sharding import PartitionSpec as P

MESH = pl.DeviceIdType.MESH
PLACES = ((0, 0), (1, 0), (0, 1), (1, 1))


def kernel(layers, pieces, total_tokens, ht_ref, og_ref, out_ref, held, grads, sums, below, above,
           og_send, og_recv, hid_send, hid_recv, up_send, up_recv, down_send, down_recv):
    gx, gy, y = lax.axis_index("gx"), lax.axis_index("gy"), lax.axis_index("gz")
    x, core = gy // 2, gy % 2
    rows, columns = out_ref.shape
    tokens = og_ref.shape[0]
    half = tokens // 2
    last = layers - 1

    def peer(flip, place):
        px = 1 - x if place[0] else x
        py = 1 - y if place[1] else y
        pc = 1 - core if flip else core
        return px, pc, py

    def device(who):
        px, pc, py = who
        return (gx, px * 2 + pc, py)

    peers = [(flip, at) for flip in range(2) for at in range(4) if (flip, at) != (0, 0)]
    barrier = pltpu.get_barrier_semaphore()
    for flip, at in peers:
        pl.semaphore_signal(barrier, inc=1, device_id=device(peer(flip, PLACES[at])), device_id_type=MESH)

    @pl.when(gx > 0)
    def _():
        pl.semaphore_signal(barrier, inc=1, device_id=(gx - 1, gy, y), device_id_type=MESH)

    @pl.when(gx < last)
    def _():
        pl.semaphore_signal(barrier, inc=1, device_id=(gx + 1, gy, y), device_id_type=MESH)

    inner = jnp.logical_and(gx > 0, gx < last)

    @pl.when(inner)
    def _():
        pl.semaphore_wait(barrier, len(peers) + 2)

    @pl.when(jnp.logical_not(inner))
    def _():
        pl.semaphore_wait(barrier, len(peers) + 1)

    def send(src, dst, send_sem, recv_sem, who):
        return pltpu.make_async_remote_copy(
            src_ref=src, dst_ref=dst, send_sem=send_sem, recv_sem=recv_sem,
            device_id=who, device_id_type=MESH)

    first, second = pl.ds(0, half), pl.ds(half, half)
    across_x, across_y = device(peer(0, PLACES[1])), device(peer(0, PLACES[2]))
    sibling = device(peer(1, PLACES[0]))

    def og_copy(index, src, dst, who):
        return send(src, dst, og_send.at[index], og_recv.at[index], who)

    to_x = og_copy(0, og_ref, grads.at[0, 1], across_x)
    to_y = og_copy(1, og_ref, grads.at[0, 2], across_y)
    diag_y = og_copy(2, grads.at[0, 1, first], grads.at[0, 3, first], across_y)
    diag_x = og_copy(3, grads.at[0, 2, second], grads.at[0, 3, second], across_x)
    to_sib = [
        og_copy(4, og_ref, grads.at[1, 0], sibling),
        og_copy(5, grads.at[0, 1], grads.at[1, 1], sibling),
        og_copy(6, grads.at[0, 2], grads.at[1, 2], sibling),
        og_copy(7, grads.at[0, 3, first], grads.at[1, 3, first], sibling),
        og_copy(8, grads.at[0, 3, second], grads.at[1, 3, second], sibling),
    ]

    def hid_copy(zb, flip, at):
        who = peer(flip, PLACES[at])
        return send(ht_ref.at[zb, who[0], who[1], who[2]], held.at[zb, flip, at],
                    hid_send.at[zb, flip, at], hid_recv.at[zb, flip, at], device(who))

    def send_hidden(zb):
        for at in (3, 1, 2, 0):
            for flip in range(2):
                if (flip, at) != (0, 0):
                    hid_copy(zb, flip, at).start()

    order = []
    for step in range((layers + 1) // 2):
        order += [last - step] if last - step == step else [last - step, step]

    to_x.start()
    to_y.start()
    to_sib[0].start()
    send_hidden(order[0])
    to_x.wait_recv()
    diag_y.start()
    to_sib[1].start()
    to_y.wait_recv()
    diag_x.start()
    to_sib[2].start()
    for zb in order[1:]:
        send_hidden(zb)
    diag_y.wait_recv()
    to_sib[3].start()
    diag_x.wait_recv()
    to_sib[4].start()
    for copy in to_sib:
        copy.wait_recv()

    width = columns // 3 if columns % 384 == 0 else columns
    piece = rows // pieces

    def up_copy(zb, k):
        part = pl.ds(k * piece, piece)
        return send(sums.at[zb, part], below.at[zb, part], up_send.at[zb, k], up_recv.at[zb, k],
                    (gx + 1, gy, y))

    def down_copy(zb, k):
        part = pl.ds(k * piece, piece)
        return send(sums.at[zb, part], above.at[zb, part], down_send.at[zb, k], down_recv.at[zb, k],
                    (gx - 1, gy, y))

    def compute(zb):
        for flip, at in peers:
            hid_copy(zb, flip, at).wait_recv()

        @pl.loop(0, columns // width)
        def _(n):
            part = pl.ds(pl.multiple_of(n * width, width), width)
            total = jnp.dot(ht_ref[zb, x, core, y], og_ref[:, part], preferred_element_type=jnp.float32)
            for flip, at in peers:
                total += jnp.dot(held[zb, flip, at], grads[flip, at, :, part],
                                 preferred_element_type=jnp.float32)
            sums[zb, :, part] = total

        if zb > 0:
            @pl.when(gx == 0)
            def _():
                for k in range(pieces):
                    up_copy(zb, k).start()
        if zb < last:
            @pl.when(gx == last)
            def _():
                for k in range(pieces):
                    down_copy(zb, k).start()

    factor = 1.0 / jnp.sqrt(jnp.float32(total_tokens))

    def relay(zb):
        if zb > 1:
            @pl.when(jnp.logical_and(gx > 0, gx < zb))
            def _():
                for k in range(pieces):
                    part = pl.ds(k * piece, piece)
                    up_copy(zb, k).wait_recv()
                    sums[zb, part] += below[zb, part]
                    up_copy(zb, k).start()
        if zb < last - 1:
            @pl.when(jnp.logical_and(gx > zb, gx < last))
            def _():
                for k in range(pieces):
                    part = pl.ds(k * piece, piece)
                    down_copy(zb, k).wait_recv()
                    sums[zb, part] += above[zb, part]
                    down_copy(zb, k).start()

    def finish(zb):
        @pl.when(gx == zb)
        def _():
            for k in range(pieces):
                part = pl.ds(k * piece, piece)
                total = sums[zb, part]
                if zb > 0:
                    up_copy(zb, k).wait_recv()
                    total += below[zb, part]
                if zb < last:
                    down_copy(zb, k).wait_recv()
                    total += above[zb, part]
                out_ref[part, :] = total * factor

    for step, zb in enumerate(order):
        compute(zb)
        if step > 0:
            relay(order[step - 1])
    relay(order[-1])
    for zb in order:
        finish(zb)

    for copy in [to_x, to_y, diag_y, diag_x] + to_sib:
        copy.wait_send()
    for zb in order:
        for flip, at in peers:
            hid_copy(zb, flip, at).wait_send()
        if zb > 0:
            @pl.when(gx < zb)
            def _():
                for k in range(pieces):
                    up_copy(zb, k).wait_send()
        if zb < last:
            @pl.when(gx > zb)
            def _():
                for k in range(pieces):
                    down_copy(zb, k).wait_send()


def body(hidden, out_grad, down_weight):
    layers = lax.axis_size("gx")
    devices = layers * lax.axis_size("gy") * lax.axis_size("gz")
    tokens, features = hidden.shape
    columns = out_grad.shape[1]
    rows = features // devices
    pieces = 3 if rows % 24 == 0 else 1
    turned = hidden.T.reshape(layers, 2, 2, 2, rows, tokens)
    vmem = pl.BlockSpec(memory_space=pltpu.VMEM)
    dma = pltpu.SemaphoreType.DMA
    weight_grad = pl.pallas_call(
        functools.partial(kernel, layers, pieces, tokens * devices),
        out_shape=jax.ShapeDtypeStruct((rows, columns), jnp.float32),
        in_specs=[vmem, vmem],
        out_specs=vmem,
        scratch_shapes=[
            pltpu.VMEM((layers, 2, 4, rows, tokens), jnp.bfloat16),
            pltpu.VMEM((2, 4, tokens, columns), jnp.bfloat16),
            pltpu.VMEM((layers, rows, columns), jnp.float32),
            pltpu.VMEM((layers, rows, columns), jnp.float32),
            pltpu.VMEM((layers, rows, columns), jnp.float32),
            dma((9,)), dma((9,)),
            dma((layers, 2, 4)), dma((layers, 2, 4)),
            dma((layers, pieces)), dma((layers, pieces)),
            dma((layers, pieces)), dma((layers, pieces)),
        ],
        compiler_params=pltpu.CompilerParams(
            collective_id=0, has_side_effects=True, vmem_limit_bytes=40 * 1024 * 1024),
        name="weight_grad",
    )(turned, out_grad)
    product = lax.dot_general(
        out_grad, down_weight, (((1,), (1,)), ((), ())), preferred_element_type=jnp.float32
    )
    return (weight_grad, product.astype(jnp.bfloat16))


def solution(mesh):
    in_specs = (P(("gx", "gy", "gz"), None), P(("gx", "gy", "gz"), None), P())
    out_specs = (P(("gx", "gy", "gz"), None), P(("gx", "gy", "gz"), None))
    return jax.shard_map(body, mesh=mesh, in_specs=in_specs, out_specs=out_specs, check_vma=False)
```

```python
import functools

import jax
import jax.numpy as jnp
from jax import lax
from jax.experimental import pallas as pl
from jax.experimental.pallas import tpu as pltpu
from jax.sharding import PartitionSpec as P

MESH = pl.DeviceIdType.MESH
PLACES = ((0, 0), (1, 0), (0, 1), (1, 1))


def kernel(layers, pieces, cuts, turn, total_tokens, hid_any, og_any, weight_any, out_ref, product_ref,
           og_ref, weight, loaded, ht_ref, held, grads, sums, below, above, load_sem,
           og_send, og_recv, hid_send, hid_recv, up_send, up_recv, down_send, down_recv):
    gx, gy, y = lax.axis_index("gx"), lax.axis_index("gy"), lax.axis_index("gz")
    x, core = gy // 2, gy % 2
    rows, columns = out_ref.shape
    tokens = og_ref.shape[0]
    half = tokens // 2
    last = layers - 1

    og_load = pltpu.make_async_copy(og_any, og_ref, load_sem.at[0])
    hid_load = pltpu.make_async_copy(hid_any, loaded if turn else ht_ref, load_sem.at[1])
    weight_load = pltpu.make_async_copy(weight_any, weight, load_sem.at[2])
    og_load.start()
    hid_load.start()
    weight_load.start()

    def peer(flip, place):
        px = 1 - x if place[0] else x
        py = 1 - y if place[1] else y
        pc = 1 - core if flip else core
        return px, pc, py

    def device(who):
        px, pc, py = who
        return (gx, px * 2 + pc, py)

    peers = [(flip, at) for flip in range(2) for at in range(4) if (flip, at) != (0, 0)]
    barrier = pltpu.get_barrier_semaphore()
    for flip, at in peers:
        pl.semaphore_signal(barrier, inc=1, device_id=device(peer(flip, PLACES[at])), device_id_type=MESH)

    @pl.when(gx > 0)
    def _():
        pl.semaphore_signal(barrier, inc=1, device_id=(gx - 1, gy, y), device_id_type=MESH)

    @pl.when(gx < last)
    def _():
        pl.semaphore_signal(barrier, inc=1, device_id=(gx + 1, gy, y), device_id_type=MESH)

    inner = jnp.logical_and(gx > 0, gx < last)

    @pl.when(inner)
    def _():
        pl.semaphore_wait(barrier, len(peers) + 2)

    @pl.when(jnp.logical_not(inner))
    def _():
        pl.semaphore_wait(barrier, len(peers) + 1)

    def send(src, dst, send_sem, recv_sem, who):
        return pltpu.make_async_remote_copy(
            src_ref=src, dst_ref=dst, send_sem=send_sem, recv_sem=recv_sem,
            device_id=who, device_id_type=MESH)

    first, second = pl.ds(0, half), pl.ds(half, half)
    across_x, across_y = device(peer(0, PLACES[1])), device(peer(0, PLACES[2]))
    sibling = device(peer(1, PLACES[0]))

    def og_copies(c):
        cols = pl.ds(*cuts[c])
        mine = og_ref.at[:, cols]
        at_x, at_y = grads.at[0, 1, :, cols], grads.at[0, 2, :, cols]
        near, far = grads.at[0, 3, first, cols], grads.at[0, 3, second, cols]
        plan = (
            (mine, at_x, across_x),
            (mine, at_y, across_y),
            (grads.at[0, 1, first, cols], near, across_y),
            (grads.at[0, 2, second, cols], far, across_x),
            (mine, grads.at[1, 0, :, cols], sibling),
            (at_x, grads.at[1, 1, :, cols], sibling),
            (at_y, grads.at[1, 2, :, cols], sibling),
            (near, grads.at[1, 3, first, cols], sibling),
            (far, grads.at[1, 3, second, cols], sibling),
        )
        return [send(src, dst, og_send.at[c, i], og_recv.at[c, i], who)
                for i, (src, dst, who) in enumerate(plan)]

    def og_begin(c):
        copies = og_copies(c)
        for i in (0, 1, 4):
            copies[i].start()

    def og_pass(c):
        copies = og_copies(c)
        for got, onward in ((0, 2), (1, 3)):
            copies[got].wait_recv()
            copies[onward].start()
            copies[got + 5].start()

    def og_end(c):
        copies = og_copies(c)
        for got in (2, 3):
            copies[got].wait_recv()
            copies[got + 5].start()
        for i in range(4, 9):
            copies[i].wait_recv()

    def hid_copy(zb, flip, at):
        who = peer(flip, PLACES[at])
        return send(ht_ref.at[zb, who[0], who[1], who[2]], held.at[zb, flip, at],
                    hid_send.at[zb, flip, at], hid_recv.at[zb, flip, at], device(who))

    def send_hidden(zb):
        for at in (3, 1, 2, 0):
            for flip in range(2):
                if (flip, at) != (0, 0):
                    hid_copy(zb, flip, at).start()

    order = []
    for step in range((layers + 1) // 2):
        order += [last - step] if last - step == step else [last - step, step]

    og_load.wait()
    og_begin(0)
    hid_load.wait()
    if turn:
        group = 8 * rows

        def turned(zb):
            block = loaded[:, zb * group:(zb + 1) * group].T
            ht_ref[zb] = block.reshape(2, 2, 2, rows, tokens)
    else:
        def turned(zb):
            pass

    turned(order[0])
    send_hidden(order[0])
    weight_load.wait()
    features = weight.shape[0]
    tile = features // layers if features % (128 * layers) == 0 else features // 9

    @pl.loop(0, features // tile)
    def _(n):
        part = pl.ds(pl.multiple_of(n * tile, tile), tile)
        product_ref[:, part] = lax.dot_general(
            og_ref[...], weight[part, :], (((1,), (1,)), ((), ())),
            preferred_element_type=jnp.float32).astype(product_ref.dtype)

    for zb in order[1:]:
        turned(zb)
    og_pass(0)
    send_hidden(order[1])
    og_end(0)

    piece = rows // pieces

    def up_copy(zb, c, k):
        part = (zb, pl.ds(k * piece, piece), pl.ds(*cuts[c]))
        return send(sums.at[part], below.at[part], up_send.at[zb, c, k], up_recv.at[zb, c, k],
                    (gx + 1, gy, y))

    def down_copy(zb, c, k):
        part = (zb, pl.ds(k * piece, piece), pl.ds(*cuts[c]))
        return send(sums.at[part], above.at[part], down_send.at[zb, c, k], down_recv.at[zb, c, k],
                    (gx - 1, gy, y))

    def compute(zb, c):
        begin, size = cuts[c]
        width = cuts[-1][1]

        @pl.loop(0, size // width)
        def _(n):
            part = pl.ds(pl.multiple_of(begin + n * width, 128), width)
            total = jnp.dot(ht_ref[zb, x, core, y], og_ref[:, part], preferred_element_type=jnp.float32)
            for flip, at in peers:
                total += jnp.dot(held[zb, flip, at], grads[flip, at, :, part],
                                 preferred_element_type=jnp.float32)
            sums[zb, :, part] = total

        if zb > 0:
            @pl.when(gx == 0)
            def _():
                for k in range(pieces):
                    up_copy(zb, c, k).start()
        if zb < last:
            @pl.when(gx == last)
            def _():
                for k in range(pieces):
                    down_copy(zb, c, k).start()

    factor = 1.0 / jnp.sqrt(jnp.float32(total_tokens))

    def relay(zb, c):
        cols = pl.ds(*cuts[c])
        if zb > 1:
            @pl.when(jnp.logical_and(gx > 0, gx < zb))
            def _():
                for k in range(pieces):
                    part = pl.ds(k * piece, piece)
                    up_copy(zb, c, k).wait_recv()
                    sums[zb, part, cols] += below[zb, part, cols]
                    up_copy(zb, c, k).start()
        if zb < last - 1:
            @pl.when(jnp.logical_and(gx > zb, gx < last))
            def _():
                for k in range(pieces):
                    part = pl.ds(k * piece, piece)
                    down_copy(zb, c, k).wait_recv()
                    sums[zb, part, cols] += above[zb, part, cols]
                    down_copy(zb, c, k).start()

    def finish(zb, c):
        cols = pl.ds(*cuts[c])

        @pl.when(gx == zb)
        def _():
            for k in range(pieces):
                part = pl.ds(k * piece, piece)
                total = sums[zb, part, cols]
                if zb > 0:
                    up_copy(zb, c, k).wait_recv()
                    total += below[zb, part, cols]
                if zb < last:
                    down_copy(zb, c, k).wait_recv()
                    total += above[zb, part, cols]
                out_ref[part, cols] = total * factor

    for step, zb in enumerate(order):
        for flip, at in peers:
            hid_copy(zb, flip, at).wait_recv()
        if step + 2 < len(order):
            send_hidden(order[step + 2])
        if step == max(len(order) - 2, 0):
            for c in range(1, len(cuts)):
                og_begin(c)
        compute(zb, 0)
        if step > 0:
            relay(order[step - 1], 0)
    for c in range(1, len(cuts)):
        og_pass(c)
        og_end(c)
        for step, zb in enumerate(order):
            compute(zb, c)
            if step == 1:
                relay(order[-1], c - 1)
        for zb in order[:-1]:
            relay(zb, c)
    relay(order[-1], len(cuts) - 1)
    for c in range(len(cuts)):
        for zb in order:
            finish(zb, c)

    for c in range(len(cuts)):
        for copy in og_copies(c):
            copy.wait_send()
    for zb in order:
        for flip, at in peers:
            hid_copy(zb, flip, at).wait_send()
        for c in range(len(cuts)):
            if zb > 0:
                @pl.when(gx < zb)
                def _():
                    for k in range(pieces):
                        up_copy(zb, c, k).wait_send()
            if zb < last:
                @pl.when(gx > zb)
                def _():
                    for k in range(pieces):
                        down_copy(zb, c, k).wait_send()


def body(hidden, out_grad, down_weight):
    layers = lax.axis_size("gx")
    devices = layers * lax.axis_size("gy") * lax.axis_size("gz")
    tokens, features = hidden.shape
    columns = out_grad.shape[1]
    rows = features // devices
    pieces = 3 if rows % 24 == 0 else 1
    third = columns // 3
    cuts = ((0, 2 * third), (2 * third, third)) if columns % 384 == 0 else ((0, columns),)
    turn = rows % 16 == 0
    shape = (layers, 2, 2, 2, rows, tokens)
    source = hidden if turn else hidden.T.reshape(shape)
    vmem = pl.BlockSpec(memory_space=pltpu.VMEM)
    anywhere = pl.BlockSpec(memory_space=pl.ANY)
    dma = pltpu.SemaphoreType.DMA
    return tuple(pl.pallas_call(
        functools.partial(kernel, layers, pieces, cuts, turn, tokens * devices),
        out_shape=(
            jax.ShapeDtypeStruct((rows, columns), jnp.float32),
            jax.ShapeDtypeStruct((tokens, features), jnp.bfloat16),
        ),
        in_specs=[anywhere] * 3,
        out_specs=(vmem, vmem),
        scratch_shapes=[
            pltpu.VMEM(out_grad.shape, jnp.bfloat16),
            pltpu.VMEM(down_weight.shape, jnp.bfloat16),
            pltpu.VMEM(hidden.shape if turn else (16, 128), jnp.bfloat16),
            pltpu.VMEM(shape, jnp.bfloat16),
            pltpu.VMEM((layers, 2, 4, rows, tokens), jnp.bfloat16),
            pltpu.VMEM((2, 4, tokens, columns), jnp.bfloat16),
            pltpu.VMEM((layers, rows, columns), jnp.float32),
            pltpu.VMEM((layers, rows, columns), jnp.float32),
            pltpu.VMEM((layers, rows, columns), jnp.float32),
            dma((3,)),
            dma((len(cuts), 9)), dma((len(cuts), 9)),
            dma((layers, 2, 4)), dma((layers, 2, 4)),
            dma((layers, len(cuts), pieces)), dma((layers, len(cuts), pieces)),
            dma((layers, len(cuts), pieces)), dma((layers, len(cuts), pieces)),
        ],
        compiler_params=pltpu.CompilerParams(
            collective_id=0, has_side_effects=True, vmem_limit_bytes=58 * 1024 * 1024),
        name="weight_grad",
    )(source, out_grad, down_weight))


def solution(mesh):
    in_specs = (P(("gx", "gy", "gz"), None), P(("gx", "gy", "gz"), None), P())
    out_specs = (P(("gx", "gy", "gz"), None), P(("gx", "gy", "gz"), None))
    return jax.shard_map(body, mesh=mesh, in_specs=in_specs, out_specs=out_specs, check_vma=False)
```

```python
import functools

import jax
import jax.numpy as jnp
from jax import lax
from jax.experimental import pallas as pl
from jax.experimental.pallas import tpu as pltpu
from jax.sharding import PartitionSpec as P

MESH = pl.DeviceIdType.MESH
PLACES = ((0, 0), (1, 0), (0, 1), (1, 1))


def kernel(layers, pieces, cuts, turn, total_tokens, hid_any, og_any, weight_any, out_ref, product_ref,
           og_ref, weight, loaded, ht_ref, held, grads, sums, below, above, load_sem,
           og_send, og_recv, hid_send, hid_recv, up_send, up_recv, down_send, down_recv):
    gx, gy, y = lax.axis_index("gx"), lax.axis_index("gy"), lax.axis_index("gz")
    x, core = gy // 2, gy % 2
    rows, columns = out_ref.shape
    tokens = og_ref.shape[0]
    half = tokens // 2
    last = layers - 1

    og_load = pltpu.make_async_copy(og_any, og_ref, load_sem.at[0])
    hid_load = pltpu.make_async_copy(hid_any, loaded if turn else ht_ref, load_sem.at[1])
    weight_load = pltpu.make_async_copy(weight_any, weight, load_sem.at[2])
    og_load.start()
    hid_load.start()
    weight_load.start()

    def peer(flip, place):
        px = 1 - x if place[0] else x
        py = 1 - y if place[1] else y
        pc = 1 - core if flip else core
        return px, pc, py

    def device(who):
        px, pc, py = who
        return (gx, px * 2 + pc, py)

    peers = [(flip, at) for flip in range(2) for at in range(4) if (flip, at) != (0, 0)]
    barrier = pltpu.get_barrier_semaphore()
    for flip, at in peers:
        pl.semaphore_signal(barrier, inc=1, device_id=device(peer(flip, PLACES[at])), device_id_type=MESH)

    @pl.when(gx > 0)
    def _():
        pl.semaphore_signal(barrier, inc=1, device_id=(gx - 1, gy, y), device_id_type=MESH)

    @pl.when(gx < last)
    def _():
        pl.semaphore_signal(barrier, inc=1, device_id=(gx + 1, gy, y), device_id_type=MESH)

    inner = jnp.logical_and(gx > 0, gx < last)

    @pl.when(inner)
    def _():
        pl.semaphore_wait(barrier, len(peers) + 2)

    @pl.when(jnp.logical_not(inner))
    def _():
        pl.semaphore_wait(barrier, len(peers) + 1)

    def send(src, dst, send_sem, recv_sem, who):
        return pltpu.make_async_remote_copy(
            src_ref=src, dst_ref=dst, send_sem=send_sem, recv_sem=recv_sem,
            device_id=who, device_id_type=MESH)

    first, second = pl.ds(0, half), pl.ds(half, half)
    across_x, across_y = device(peer(0, PLACES[1])), device(peer(0, PLACES[2]))
    sibling = device(peer(1, PLACES[0]))

    def og_copies(c):
        cols = pl.ds(*cuts[c])
        mine = og_ref.at[:, cols]
        at_x, at_y = grads.at[0, 1, :, cols], grads.at[0, 2, :, cols]
        near, far = grads.at[0, 3, first, cols], grads.at[0, 3, second, cols]
        plan = (
            (mine, at_x, across_x),
            (mine, at_y, across_y),
            (grads.at[0, 1, first, cols], near, across_y),
            (grads.at[0, 2, second, cols], far, across_x),
            (mine, grads.at[1, 0, :, cols], sibling),
            (at_x, grads.at[1, 1, :, cols], sibling),
            (at_y, grads.at[1, 2, :, cols], sibling),
            (near, grads.at[1, 3, first, cols], sibling),
            (far, grads.at[1, 3, second, cols], sibling),
        )
        return [send(src, dst, og_send.at[c, i], og_recv.at[c, i], who)
                for i, (src, dst, who) in enumerate(plan)]

    def og_begin(c):
        copies = og_copies(c)
        for i in (0, 1, 4):
            copies[i].start()

    def og_pass(c):
        copies = og_copies(c)
        for got, onward in ((0, 2), (1, 3)):
            copies[got].wait_recv()
            copies[onward].start()
            copies[got + 5].start()

    def og_end(c):
        copies = og_copies(c)
        for got in (2, 3):
            copies[got].wait_recv()
            copies[got + 5].start()
        for i in range(4, 9):
            copies[i].wait_recv()

    def hid_copy(zb, flip, at):
        who = peer(flip, PLACES[at])
        return send(ht_ref.at[zb, who[0], who[1], who[2]], held.at[zb, flip, at],
                    hid_send.at[zb, flip, at], hid_recv.at[zb, flip, at], device(who))

    def send_hidden(zb):
        for at in (3, 1, 2, 0):
            for flip in range(2):
                if (flip, at) != (0, 0):
                    hid_copy(zb, flip, at).start()

    order = []
    for step in range((layers + 1) // 2):
        order += [last - step] if last - step == step else [last - step, step]

    og_load.wait()
    og_begin(0)
    hid_load.wait()
    if turn:
        group = 8 * rows

        def turned(zb):
            block = loaded[:, zb * group:(zb + 1) * group].T
            ht_ref[zb] = block.reshape(2, 2, 2, rows, tokens)
    else:
        def turned(zb):
            pass

    turned(order[0])
    weight_load.wait()
    features = weight.shape[0]
    tile = features // layers if features % (128 * layers) == 0 else features // 9

    @pl.loop(0, features // tile)
    def _(n):
        part = pl.ds(pl.multiple_of(n * tile, tile), tile)
        product_ref[:, part] = lax.dot_general(
            og_ref[...], weight[part, :], (((1,), (1,)), ((), ())),
            preferred_element_type=jnp.float32).astype(product_ref.dtype)

    for zb in order[1:]:
        turned(zb)
    og_pass(0)
    send_hidden(order[0])
    send_hidden(order[1])
    og_end(0)

    piece = rows // pieces

    def up_copy(zb, c, k):
        part = (zb, pl.ds(k * piece, piece), pl.ds(*cuts[c]))
        return send(sums.at[part], below.at[part], up_send.at[zb, c, k], up_recv.at[zb, c, k],
                    (gx + 1, gy, y))

    def down_copy(zb, c, k):
        part = (zb, pl.ds(k * piece, piece), pl.ds(*cuts[c]))
        return send(sums.at[part], above.at[part], down_send.at[zb, c, k], down_recv.at[zb, c, k],
                    (gx - 1, gy, y))

    def compute(zb, c):
        begin, size = cuts[c]
        width = cuts[-1][1]

        @pl.loop(0, size // width)
        def _(n):
            part = pl.ds(pl.multiple_of(begin + n * width, 128), width)
            total = jnp.dot(ht_ref[zb, x, core, y], og_ref[:, part], preferred_element_type=jnp.float32)
            for flip, at in peers:
                total += jnp.dot(held[zb, flip, at], grads[flip, at, :, part],
                                 preferred_element_type=jnp.float32)
            sums[zb, :, part] = total

        if zb > 0:
            @pl.when(gx == 0)
            def _():
                for k in range(pieces):
                    up_copy(zb, c, k).start()
        if zb < last:
            @pl.when(gx == last)
            def _():
                for k in range(pieces):
                    down_copy(zb, c, k).start()

    factor = 1.0 / jnp.sqrt(jnp.float32(total_tokens))

    def relay(zb, c):
        cols = pl.ds(*cuts[c])
        if zb > 1:
            @pl.when(jnp.logical_and(gx > 0, gx < zb))
            def _():
                for k in range(pieces):
                    part = pl.ds(k * piece, piece)
                    up_copy(zb, c, k).wait_recv()
                    sums[zb, part, cols] += below[zb, part, cols]
                    up_copy(zb, c, k).start()
        if zb < last - 1:
            @pl.when(jnp.logical_and(gx > zb, gx < last))
            def _():
                for k in range(pieces):
                    part = pl.ds(k * piece, piece)
                    down_copy(zb, c, k).wait_recv()
                    sums[zb, part, cols] += above[zb, part, cols]
                    down_copy(zb, c, k).start()

    def finish(zb, c):
        cols = pl.ds(*cuts[c])

        @pl.when(gx == zb)
        def _():
            for k in range(pieces):
                part = pl.ds(k * piece, piece)
                total = sums[zb, part, cols]
                if zb > 0:
                    up_copy(zb, c, k).wait_recv()
                    total += below[zb, part, cols]
                if zb < last:
                    down_copy(zb, c, k).wait_recv()
                    total += above[zb, part, cols]
                out_ref[part, cols] = total * factor

    for step, zb in enumerate(order):
        for flip, at in peers:
            hid_copy(zb, flip, at).wait_recv()
        if step + 2 < len(order):
            send_hidden(order[step + 2])
        if step == max(len(order) - 2, 0):
            for c in range(1, len(cuts)):
                og_begin(c)
        compute(zb, 0)
        if step > 0:
            relay(order[step - 1], 0)
    for c in range(1, len(cuts)):
        og_pass(c)
        og_end(c)
        for step, zb in enumerate(order):
            compute(zb, c)
            if step == 1:
                relay(order[-1], c - 1)
        for zb in order[:-1]:
            relay(zb, c)
    relay(order[-1], len(cuts) - 1)
    for c in range(len(cuts)):
        for zb in order:
            finish(zb, c)

    for c in range(len(cuts)):
        for copy in og_copies(c):
            copy.wait_send()
    for zb in order:
        for flip, at in peers:
            hid_copy(zb, flip, at).wait_send()
        for c in range(len(cuts)):
            if zb > 0:
                @pl.when(gx < zb)
                def _():
                    for k in range(pieces):
                        up_copy(zb, c, k).wait_send()
            if zb < last:
                @pl.when(gx > zb)
                def _():
                    for k in range(pieces):
                        down_copy(zb, c, k).wait_send()


def body(hidden, out_grad, down_weight):
    layers = lax.axis_size("gx")
    devices = layers * lax.axis_size("gy") * lax.axis_size("gz")
    tokens, features = hidden.shape
    columns = out_grad.shape[1]
    rows = features // devices
    pieces = 3 if rows % 24 == 0 else 1
    third = columns // 3
    cuts = ((0, 2 * third), (2 * third, third)) if columns % 384 == 0 else ((0, columns),)
    turn = rows % 16 == 0
    shape = (layers, 2, 2, 2, rows, tokens)
    source = hidden if turn else hidden.T.reshape(shape)
    vmem = pl.BlockSpec(memory_space=pltpu.VMEM)
    anywhere = pl.BlockSpec(memory_space=pl.ANY)
    dma = pltpu.SemaphoreType.DMA
    return tuple(pl.pallas_call(
        functools.partial(kernel, layers, pieces, cuts, turn, tokens * devices),
        out_shape=(
            jax.ShapeDtypeStruct((rows, columns), jnp.float32),
            jax.ShapeDtypeStruct((tokens, features), jnp.bfloat16),
        ),
        in_specs=[anywhere] * 3,
        out_specs=(vmem, vmem),
        scratch_shapes=[
            pltpu.VMEM(out_grad.shape, jnp.bfloat16),
            pltpu.VMEM(down_weight.shape, jnp.bfloat16),
            pltpu.VMEM(hidden.shape if turn else (16, 128), jnp.bfloat16),
            pltpu.VMEM(shape, jnp.bfloat16),
            pltpu.VMEM((layers, 2, 4, rows, tokens), jnp.bfloat16),
            pltpu.VMEM((2, 4, tokens, columns), jnp.bfloat16),
            pltpu.VMEM((layers, rows, columns), jnp.float32),
            pltpu.VMEM((layers, rows, columns), jnp.float32),
            pltpu.VMEM((layers, rows, columns), jnp.float32),
            dma((3,)),
            dma((len(cuts), 9)), dma((len(cuts), 9)),
            dma((layers, 2, 4)), dma((layers, 2, 4)),
            dma((layers, len(cuts), pieces)), dma((layers, len(cuts), pieces)),
            dma((layers, len(cuts), pieces)), dma((layers, len(cuts), pieces)),
        ],
        compiler_params=pltpu.CompilerParams(
            collective_id=0, has_side_effects=True, vmem_limit_bytes=44 * 1024 * 1024),
        name="weight_grad",
    )(source, out_grad, down_weight))


def solution(mesh):
    in_specs = (P(("gx", "gy", "gz"), None), P(("gx", "gy", "gz"), None), P())
    out_specs = (P(("gx", "gy", "gz"), None), P(("gx", "gy", "gz"), None))
    return jax.shard_map(body, mesh=mesh, in_specs=in_specs, out_specs=out_specs, check_vma=False)
```
